32 devices in a mesh: prompts: 2 (over x), beam: 16 (over z, y, core).
Axes of the slice: x: 2, y: 2, z: 4, core: 2. Of those that a mesh axis runs over, the one named last changes fastest.
Arguments:
- queries: bfloat16 [128, 256, 4096], P(('prompts', 'beam')), parts along dimension 0, may hold values from -4.375 to 4.375
- new_keys: bfloat16 [128, 256, 1024], P(('prompts', 'beam')), parts along dimension 0, may hold values from -4.375 to 4.375
- new_values: bfloat16 [128, 256, 1024], P(('prompts', 'beam')), parts along dimension 0, may hold values from -6 to 6
- step_kv: bfloat16 [128, 2, 64, 1024], P(('prompts', 'beam')), parts along dimension 0, may hold values from -6 to 6
- prm_last: bfloat16 [128, 4096], P(('prompts', 'beam')), parts along dimension 0, may hold values from -6 to 6
- value_head: float32 [4096], replicated, may hold values from -0.09375 to 0.09375
- parents: int32 [128], P('prompts'), parts along dimension 0, may hold values from 0 to 63, as said below
Outputs:
- attended: bfloat16 [128, 256, 4096], P(('prompts', 'beam')), parts along dimension 0
- child_share: float32 [128], P(('prompts', 'beam')), parts along dimension 0
The draws below stay inside these ranges and needn't reach their ends.
There are 2 independent parts, one for each index of `prompts`. The reference program is written for one: setup_inputs(seed, part) draws one part's arguments, and reference() takes and returns one part's arrays. A program takes and returns all parts, laid end to end along the dimension named above; an argument that names none is the same for every part. Nothing has to cross between parts.
Inputs may be any that keep to these rules, and one draw needn't show every extreme that they name: `parents`: on every device exactly 2 of its 4 beams are the parent of one or more children and the other beams of none.
All inputs are finite; a program needn't handle non-finite values.
Results may differ from the reference program's by a relative error of at most 0.008.
Values may be sent and summed in bfloat16 or wider, within the bound.
A program may use at most 192 MiB of HBM per device.

```python
import jax
import jax.numpy as jnp
from jax import lax

D = 4096
HEADS = 32
KV_HEADS = 8
HEAD_SIZE = 128
NEW = 256
STEP = 64
BEAM_DEV = 4
KEEP = 2
BEAMS = 64
CHILDREN = 64


def drawn_pair(key):
    base = jax.random.fold_in(key, 7919)
    key_q, key_k = jax.random.split(base, 2)
    q_shape = (CHILDREN, NEW, HEADS * HEAD_SIZE)
    k_shape = (CHILDREN, NEW, KV_HEADS * HEAD_SIZE)
    queries = jnp.clip(jax.random.normal(key_q, q_shape, jnp.float32), -4.375, 4.375)
    keys = jnp.clip(jax.random.normal(key_k, k_shape, jnp.float32), -4.375, 4.375)
    return (queries, keys)


def draw_queries(key, part):
    return drawn_pair(key)[0].astype(jnp.bfloat16)


def draw_new_keys(key, part):
    return drawn_pair(key)[1].astype(jnp.bfloat16)


def draw_parents(key, part):
    base = jax.random.fold_in(key, 5303)
    key_a, key_b, key_c, key_d, key_e = jax.random.split(base, 5)
    groups = BEAMS // BEAM_DEV
    ranks = jax.random.randint(key_a, (groups, BEAM_DEV), 0, 1048576) * BEAM_DEV + jnp.arange(BEAM_DEV)[None, :]
    order = jnp.argsort(ranks, axis=1, stable=True)
    kept_beams = (jnp.arange(groups)[:, None] * BEAM_DEV + order[:, :KEEP]).reshape(-1)
    kept_count = groups * KEEP
    shuffled = jax.random.permutation(key_b, kept_beams)
    extra = CHILDREN - kept_count
    upper = jax.random.randint(key_c, (extra,), 1, kept_count + 1)
    picks = jax.random.randint(key_d, (extra,), 0, upper)
    assign = jnp.concatenate([shuffled, shuffled[picks]])
    return jax.random.permutation(key_e, assign).astype(jnp.int32)


def shard_levels(rng, dims, cuts, smallest, high):
    level, own = 1.0, jax.random.fold_in(rng, 6)
    for position, parts in cuts:
        draws = jnp.exp(jax.random.uniform(jax.random.fold_in(own, position), (parts,), jnp.float32, smallest / len(cuts), high / len(cuts)))
        level = level * jnp.repeat(draws, dims[position] // parts).reshape([-1 if axis == position else 1 for axis in range(len(dims))])
    return level


def centred(key, dims, deviation, most, cuts=(), held_as=jnp.bfloat16):
    level = shard_levels(key, dims, cuts, -0.22, 0.18) if cuts else 1.0
    entries = jax.random.normal(key, dims, jnp.float32) * deviation * level
    return jnp.minimum(jnp.maximum(entries, -most), most).astype(held_as)


def setup_inputs(seed: int = 0, part: int = 0) -> dict:
    key_list = jax.random.split(jax.random.key(seed), 8)
    part_keys = jax.random.split(jax.random.fold_in(key_list[7], part), 8)
    queries = draw_queries(jax.random.fold_in(jax.random.fold_in(key_list[7], part), 71), part)
    new_keys = draw_new_keys(jax.random.fold_in(jax.random.fold_in(key_list[7], part), 71), part)
    new_values = centred(part_keys[2], (CHILDREN, NEW, KV_HEADS * HEAD_SIZE), 1.0, 6.0, ((0, 16),))
    step_kv = centred(part_keys[3], (BEAMS, 2, STEP, KV_HEADS * HEAD_SIZE), 1.0, 6.0, ((0, 16),))
    prm_last = centred(part_keys[4], (BEAMS, D), 1.0, 6.0, ((0, 16),))
    value_head = centred(key_list[5], (D,), D ** -0.5, 0.09375, (), jnp.float32)
    parents = draw_parents(jax.random.fold_in(jax.random.fold_in(key_list[7], part), 71), part)
    return dict(queries=queries, new_keys=new_keys, new_values=new_values, step_kv=step_kv, prm_last=prm_last, value_head=value_head, parents=parents)


def attend_child(operands):
    query, keys, values = operands
    total_len = keys.shape[0]
    new_len = query.shape[0]
    step_len = total_len - new_len
    kv_width = keys.shape[1]
    kv_heads = kv_width // HEAD_SIZE
    group = query.shape[1] // kv_width
    query_head_rows = query.astype(jnp.float32).reshape(new_len, kv_heads, group, HEAD_SIZE)
    key_head_rows = keys.astype(jnp.float32).reshape(total_len, kv_heads, HEAD_SIZE)
    value_head_rows = values.astype(jnp.float32).reshape(total_len, kv_heads, HEAD_SIZE)
    attention_scores = jnp.einsum('yfli,xfi->flyx', query_head_rows, key_head_rows) * HEAD_SIZE ** (-0.5)
    column = jnp.arange(total_len)[None, :]
    row_pos = jnp.arange(new_len)[:, None]
    visible = (column < step_len) | (column - step_len <= row_pos)
    attention_scores = jnp.where(visible, attention_scores, -jnp.inf)
    attention_weights = jax.nn.softmax(attention_scores, axis=-1).astype(jnp.bfloat16).astype(jnp.float32)
    attended_values = jnp.einsum('fjip,pfa->ifja', attention_weights, value_head_rows)
    return attended_values.reshape(new_len, -1).astype(jnp.bfloat16)

def reference(queries, new_keys, new_values, step_kv, prm_last, value_head, parents):
    hidden = prm_last.astype(jnp.float32)
    square = lax.optimization_barrier(jnp.mean(hidden * hidden, axis=-1, keepdims=True))
    normed = hidden * lax.rsqrt(square + 1e-05)
    score = jnp.dot(normed, value_head, precision=lax.Precision.HIGHEST)
    reward = jax.nn.sigmoid(score).astype(jnp.bfloat16)
    child_reward = jnp.take(reward, parents, axis=0).astype(jnp.float32)
    total = jnp.sum(child_reward)
    child_share = CHILDREN * child_reward / total
    copied = jnp.take(step_kv, parents, axis=0)
    keys_all = jnp.concatenate([copied[:, 0], new_keys], axis=1)
    values_all = jnp.concatenate([copied[:, 1], new_values], axis=1)
    attended = lax.map(attend_child, (queries, keys_all, values_all))
    return (attended, child_share)
```

```python
import functools

import jax
import jax.numpy as jnp
from jax import lax
from jax.experimental import pallas as pl
from jax.experimental.pallas import tpu as pltpu
from jax.sharding import PartitionSpec as P

HEAD_SIZE = 128
KEEP = 2
LOG2E = 1.4426950408889634


def remote(src, dst, send, recv, device):
    return pltpu.make_async_remote_copy(
        src_ref=src, dst_ref=dst, send_sem=send, recv_sem=recv,
        device_id={"beam": device}, device_id_type=pl.DeviceIdType.MESH,
    )


def kernel(
    n, ny, nz, idx, prm, head, kv, q_hbm, nk_hbm, nv_hbm, out_hbm, rbuf,
    col, pbuf, ybuf, qbuf, kbuf, vbuf, obuf,
    rsend, rrecv, zsend, zrecv, csend, crecv, ysend, yrecv, isem, osem,
):
    me = lax.axis_index("beam")
    my_c = lax.rem(me, 2)
    my_y = lax.rem(lax.div(me, 2), ny)
    my_z = lax.div(me, 2 * ny)
    local = kv.shape[0]
    step_len = kv.shape[2]
    heads = kv.shape[3] // HEAD_SIZE
    new_len = q_hbm.shape[1]
    width = q_hbm.shape[2] // heads
    group = width // HEAD_SIZE
    half = new_len // 2

    def at(z, y, c):
        return (z * ny + y) * 2 + c

    core_peer = at(my_z, my_y, 1 - my_c)
    y_peer = at(my_z, lax.rem(my_y + 1, ny), my_c)

    barrier = pltpu.get_barrier_semaphore()

    def greet(d, carry):
        pl.semaphore_signal(
            barrier, inc=1, device_id={"beam": lax.rem(me + d, n)},
            device_id_type=pl.DeviceIdType.MESH,
        )
        return carry

    lax.fori_loop(1, n, greet, 0)

    def loads(k):
        cols = pl.ds(pl.multiple_of(k * HEAD_SIZE, HEAD_SIZE), HEAD_SIZE)
        wide = pl.ds(pl.multiple_of(k * width, width), width)
        lo, hi = pl.ds(0, half), pl.ds(half, half)
        return [
            pltpu.make_async_copy(q_hbm.at[:, :, wide], qbuf.at[k], isem.at[k, 0]),
            pltpu.make_async_copy(nk_hbm.at[:, hi, cols], kbuf.at[k, :, lo], isem.at[k, 1]),
            pltpu.make_async_copy(nk_hbm.at[:, lo, cols], kbuf.at[k, :, hi], isem.at[k, 2]),
            pltpu.make_async_copy(nv_hbm.at[:, hi, cols], vbuf.at[k, :, lo], isem.at[k, 3]),
            pltpu.make_async_copy(nv_hbm.at[:, lo, cols], vbuf.at[k, :, hi], isem.at[k, 4]),
        ]

    def load(k, carry):
        for copy in loads(k):
            copy.start()
        return carry

    lax.fori_loop(0, heads, load, 0)

    for k in range(heads):
        cols = slice(k * HEAD_SIZE, (k + 1) * HEAD_SIZE)
        for r in range(KEEP):
            tile = kv[0, :, :, cols]
            for b in range(1, local):
                tile = jnp.where(idx[r] == b, kv[b, :, :, cols], tile)
            col[k, 0, my_z, r] = tile

    hidden = prm[...].astype(jnp.float32)
    square = jnp.mean(hidden * hidden, axis=-1, keepdims=True)
    normed = hidden * lax.rsqrt(square + 1e-05)
    score = jnp.sum(normed * head[...], axis=-1, keepdims=True)
    reward = (1.0 / (1.0 + jnp.exp(-score))).astype(jnp.bfloat16).astype(jnp.float32)
    rbuf[me] = jnp.broadcast_to(reward, (local, 128))

    pl.semaphore_wait(barrier, n - 1)

    def z_copy(k, d):
        zt = lax.rem(my_z + d, nz)
        return remote(
            col.at[k, 0, my_z], col.at[k, 0, my_z],
            zsend.at[k, d], zrecv.at[k, my_z], at(zt, my_y, my_c),
        )

    def z_arrival(k, d):
        zs = lax.rem(my_z + d, nz)
        return remote(
            col.at[k, 0, zs], col.at[k, 0, zs],
            zsend.at[k, d], zrecv.at[k, zs], at(zs, my_y, my_c),
        )

    def z_start(k, carry):
        for d in range(1, nz):
            z_copy(k, d).start()
        return carry

    def r_copy(d):
        return remote(rbuf.at[me], rbuf.at[me], rsend.at[d], rrecv.at[me], lax.rem(me + d, n))

    def r_arrival(d):
        src = lax.rem(me + d, n)
        return remote(rbuf.at[src], rbuf.at[src], rsend.at[d], rrecv.at[src], src)

    lax.fori_loop(0, heads, z_start, 0)

    def r_start(d, carry):
        r_copy(d).start()
        return carry

    lax.fori_loop(1, n, r_start, 0)

    def c_copy(k):
        return remote(col.at[k, 0], col.at[k, 1], csend.at[k], crecv.at[k], core_peer)

    def y_copy(k):
        return remote(pbuf.at[k], ybuf.at[k], ysend.at[k], yrecv.at[k], y_peer)

    def pick(k, code, base):
        tile = base
        for c in range(2):
            for z in range(nz):
                for r in range(KEEP):
                    tile = jnp.where(code == (c * nz + z) * KEEP + r, col[k, c, z, r], tile)
        return tile

    def exchange_one(k):
        for d in range(1, nz):
            z_arrival(k, d).wait_recv()
        c_copy(k).start()

    def exchange_two(k):
        c_copy(k).wait_recv()
        if ny > 1:
            for j in range(local):
                code = idx[KEEP + local + j]
                pbuf[k, j] = pick(k, code, col[k, 0, 0, 0])
            y_copy(k).start()

    def place(k):
        if ny > 1:
            y_copy(k).wait_recv()
        for j in range(local):
            base = ybuf[k, j] if ny > 1 else col[k, 0, 0, 0]
            tile = pick(k, idx[KEEP + j], base)
            kbuf[k, j, new_len:] = tile[0]
            vbuf[k, j, new_len:] = tile[1]

    row = lax.broadcasted_iota(jnp.int32, (half, half), 0)
    column = lax.broadcasted_iota(jnp.int32, (half, half), 1)
    visible = column <= row
    scale = HEAD_SIZE ** (-0.5) * LOG2E

    def attend(k, j):
        for part in range(2):
            start = half if part == 0 else 0
            keys = kbuf[k, j, start:]
            values = vbuf[k, j, start:]
            values = jnp.concatenate([values, jnp.ones_like(values)], axis=1)
            for g in range(group):
                span = slice(g * HEAD_SIZE, (g + 1) * HEAD_SIZE)
                query = qbuf[k, j, part * half:(part + 1) * half, span]
                s = lax.dot_general(
                    query, keys, (((1,), (1,)), ((), ())), preferred_element_type=jnp.float32
                )
                s = jnp.concatenate(
                    [jnp.where(visible, s[:, :half], -jnp.inf), s[:, half:]], axis=1
                )
                top = jnp.max(s, axis=1, keepdims=True)
                p = jnp.exp2((s - top) * scale).astype(jnp.bfloat16)
                o = jnp.dot(p, values, preferred_element_type=jnp.float32)
                o = o[:, :HEAD_SIZE] / o[:, HEAD_SIZE:]
                obuf[k, j, part * half:(part + 1) * half, span] = o.astype(jnp.bfloat16)

    def o_copy(k):
        wide = pl.ds(pl.multiple_of(k * width, width), width)
        return pltpu.make_async_copy(obuf.at[k], out_hbm.at[:, :, wide], osem.at[k])

    def attend_some(k, first, last):
        def one(j, carry):
            attend(k, j)
            return carry

        lax.fori_loop(first, last, one, 0)

    def ready(k):
        for copy in loads(k):
            copy.wait()
        place(k)

    exchange_one(0)
    exchange_two(0)

    def step(k, carry):
        exchange_one(k)
        ready(k - 1)
        attend_some(k - 1, 0, local // 2)
        exchange_two(k)
        attend_some(k - 1, local // 2, local)
        o_copy(k - 1).start()
        return carry

    lax.fori_loop(1, heads, step, 0)
    ready(heads - 1)
    attend_some(heads - 1, 0, local)
    o_copy(heads - 1).start()

    def finish(k, carry):
        o_copy(k).wait()
        for d in range(1, nz):
            z_copy(k, d).wait_send()
        c_copy(k).wait_send()
        if ny > 1:
            y_copy(k).wait_send()
        return carry

    lax.fori_loop(0, heads, finish, 0)

    def r_finish(d, carry):
        r_arrival(d).wait_recv()
        r_copy(d).wait_send()
        return carry

    lax.fori_loop(1, n, r_finish, 0)


def body(queries, new_keys, new_values, step_kv, prm_last, value_head, parents):
    n = lax.axis_size("beam")
    ny = 2 if n == 16 else 1
    nz = n // (2 * ny)
    me = lax.axis_index("beam")
    local, new_len, qwidth = queries.shape
    children = parents.shape[0]
    step_len, kv_width = step_kv.shape[2:]
    heads = kv_width // HEAD_SIZE
    width = qwidth // heads

    beams = jnp.arange(n * local, dtype=jnp.int32)
    equal = parents[None, :] == beams[:, None]
    hits = jnp.sum(equal.astype(jnp.int32), axis=1)
    kept = (hits > 0).astype(jnp.int32)
    before = jnp.sum(kept[None, :] * (beams[None, :] < beams[:, None]), axis=1)
    rank_of_beam = before % KEEP
    wanted = (
        (beams[None, :] // local == me)
        & (kept[None, :] > 0)
        & (rank_of_beam[None, :] == jnp.arange(KEEP, dtype=jnp.int32)[:, None])
    )
    keep_pos = jnp.sum(wanted * (beams % local)[None, :], axis=1).astype(jnp.int32)
    rank = jnp.sum(equal * rank_of_beam[:, None], axis=0)
    owner = parents // local
    c, y, z = owner % 2, (owner // 2) % ny, owner // (2 * ny)
    my_c, my_y = me % 2, (me // 2) % ny
    code = jnp.where(y == my_y, ((c != my_c) * nz + z) * KEEP + rank, -1).astype(jnp.int32)
    y_peer = me + 2 - 4 * my_y if ny > 1 else me
    own = lax.dynamic_slice_in_dim(code, me * local, local)
    other = lax.dynamic_slice_in_dim(code, y_peer * local, local)
    idx = jnp.concatenate([keep_pos, own, other])

    dma = pltpu.SemaphoreType.DMA
    bf16 = jnp.bfloat16
    vmem = pl.BlockSpec(memory_space=pltpu.VMEM)
    anywhere = pl.BlockSpec(memory_space=pl.ANY)
    attended, rewards = pl.pallas_call(
        functools.partial(kernel, n, ny, nz),
        out_shape=(
            jax.ShapeDtypeStruct(queries.shape, bf16),
            jax.ShapeDtypeStruct((n, local, 128), jnp.float32),
        ),
        in_specs=[pl.BlockSpec(memory_space=pltpu.SMEM), vmem, vmem, vmem]
        + [anywhere] * 3,
        out_specs=(anywhere, vmem),
        scratch_shapes=[
            pltpu.VMEM((heads, 2, nz, KEEP, 2, step_len, HEAD_SIZE), bf16),
            pltpu.VMEM((heads, local, 2, step_len, HEAD_SIZE), bf16),
            pltpu.VMEM((heads, local, 2, step_len, HEAD_SIZE), bf16),
            pltpu.VMEM((heads, local, new_len, width), bf16),
            pltpu.VMEM((heads, local, new_len + step_len, HEAD_SIZE), bf16),
            pltpu.VMEM((heads, local, new_len + step_len, HEAD_SIZE), bf16),
            pltpu.VMEM((heads, local, new_len, width), bf16),
            dma((n,)), dma((n,)),
            dma((heads, nz)), dma((heads, nz)),
            dma((heads,)), dma((heads,)),
            dma((heads,)), dma((heads,)),
            dma((heads, 5)), dma((heads,)),
        ],
        compiler_params=pltpu.CompilerParams(
            collective_id=0, has_side_effects=True, vmem_limit_bytes=56 << 20
        ),
    )(idx, prm_last, value_head.reshape(1, -1), step_kv, queries, new_keys, new_values)

    reward = rewards[:, :, 0].reshape(-1)
    total = jnp.sum(reward * hits.astype(jnp.float32))
    mine = lax.dynamic_slice_in_dim(parents, me * local, local)
    match = mine[:, None] == beams[None, :]
    child_reward = jnp.sum(jnp.where(match, reward[None, :], 0.0), axis=1)
    child_share = children * child_reward / total
    return (attended, child_share)


def solution(mesh):
    in_specs = (
        P(("prompts", "beam"), None, None),
        P(("prompts", "beam"), None, None),
        P(("prompts", "beam"), None, None),
        P(("prompts", "beam"), None, None, None),
        P(("prompts", "beam"), None),
        P(),
        P("prompts"),
    )
    out_specs = (P(("prompts", "beam"), None, None), P(("prompts", "beam")))
    return jax.shard_map(body, mesh=mesh, in_specs=in_specs, out_specs=out_specs, check_vma=False)
```

```python
import functools

import jax
import jax.numpy as jnp
from jax import lax
from jax.experimental import pallas as pl
from jax.experimental.pallas import tpu as pltpu
from jax.sharding import PartitionSpec as P

HEAD_SIZE = 128
KEEP = 2
LOG2E = 1.4426950408889634


def remote(src, dst, send, recv, device):
    return pltpu.make_async_remote_copy(
        src_ref=src, dst_ref=dst, send_sem=send, recv_sem=recv,
        device_id={"beam": device}, device_id_type=pl.DeviceIdType.MESH,
    )


def kernel(
    n, ny, nz, idx, prm, head, kv, q_hbm, nk_hbm, nv_hbm, out_hbm, rbuf,
    col, pbuf, ybuf, qbuf, kbuf, vbuf, obuf,
    rsend, rrecv, zsend, zrecv, lsend, csend, crecv, ysend, yrecv, isem, osem,
):
    me = lax.axis_index("beam")
    my_c = lax.rem(me, 2)
    my_y = lax.rem(lax.div(me, 2), ny)
    my_z = lax.div(me, 2 * ny)
    local = kv.shape[0]
    step_len = kv.shape[2]
    heads = kv.shape[3] // HEAD_SIZE
    new_len = q_hbm.shape[1]
    width = q_hbm.shape[2] // heads
    group = width // HEAD_SIZE
    half = new_len // 2

    def at(z, y, c):
        return (z * ny + y) * 2 + c

    core_peer = at(my_z, my_y, 1 - my_c)
    y_peer = at(my_z, lax.rem(my_y + 1, ny), my_c)

    barrier = pltpu.get_barrier_semaphore()

    def greet(d, carry):
        pl.semaphore_signal(
            barrier, inc=1, device_id={"beam": lax.rem(me + d, n)},
            device_id_type=pl.DeviceIdType.MESH,
        )
        return carry

    lax.fori_loop(1, n, greet, 0)

    def loads(k):
        cols = pl.ds(pl.multiple_of(k * HEAD_SIZE, HEAD_SIZE), HEAD_SIZE)
        wide = pl.ds(pl.multiple_of(k * width, width), width)
        lo, hi = pl.ds(0, half), pl.ds(half, half)
        return [
            pltpu.make_async_copy(q_hbm.at[:, :, wide], qbuf.at[k], isem.at[k, 0]),
            pltpu.make_async_copy(nk_hbm.at[:, hi, cols], kbuf.at[k, :, lo], isem.at[k, 1]),
            pltpu.make_async_copy(nk_hbm.at[:, lo, cols], kbuf.at[k, :, hi], isem.at[k, 2]),
            pltpu.make_async_copy(nv_hbm.at[:, hi, cols], vbuf.at[k, :, lo], isem.at[k, 3]),
            pltpu.make_async_copy(nv_hbm.at[:, lo, cols], vbuf.at[k, :, hi], isem.at[k, 4]),
        ]

    def load(k, carry):
        for copy in loads(k):
            copy.start()
        return carry

    lax.fori_loop(0, heads, load, 0)

    for k in range(heads):
        cols = slice(k * HEAD_SIZE, (k + 1) * HEAD_SIZE)
        for r in range(KEEP):
            tile = kv[0, :, :, cols]
            for b in range(1, local):
                tile = jnp.where(idx[r] == b, kv[b, :, :, cols], tile)
            col[k, 0, my_z, r] = tile

    hidden = prm[...].astype(jnp.float32)
    square = jnp.mean(hidden * hidden, axis=-1, keepdims=True)
    normed = hidden * lax.rsqrt(square + 1e-05)
    score = jnp.sum(normed * head[...], axis=-1, keepdims=True)
    reward = (1.0 / (1.0 + jnp.exp(-score))).astype(jnp.bfloat16).astype(jnp.float32)
    rbuf[me] = jnp.broadcast_to(reward, (local, 128))

    pl.semaphore_wait(barrier, n - 1)

    def z_copy(k, d):
        zt = lax.rem(my_z + d, nz)
        return remote(
            col.at[k, 0, my_z], col.at[k, 0, my_z],
            zsend.at[k, d], zrecv.at[k, my_z], at(zt, my_y, my_c),
        )

    def z_arrival(k, d):
        zs = lax.rem(my_z + d, nz)
        return remote(
            col.at[k, 0, zs], col.at[k, 0, zs],
            zsend.at[k, d], zrecv.at[k, zs], at(zs, my_y, my_c),
        )

    relayed = nz == 4

    def when_direct(d, run):
        if relayed and d == 1:
            pl.when(my_z != nz - 1)(run)
        elif relayed and d == nz - 1:
            pl.when(my_z != 0)(run)
        else:
            run()

    def relay_copy(k, source, target):
        return remote(
            col.at[k, 0, source], col.at[k, 0, source],
            lsend.at[k], zrecv.at[k, source], at(target, my_y, my_c),
        )

    ends = ((nz - 2, 0, nz - 1), (1, nz - 1, 0)) if relayed else ()

    def relay(k):
        for who, source, target in ends:

            @pl.when(my_z == who)
            def _():
                relay_copy(k, source, target).wait_recv()
                relay_copy(k, source, target).start()

    def z_wait(k):
        for d in range(1, nz):
            zs = lax.rem(my_z + d, nz)
            got = (my_z == 1) & (zs == nz - 1) | (my_z == nz - 2) & (zs == 0)
            if relayed:

                @pl.when(jnp.logical_not(got))
                def _():
                    z_arrival(k, d).wait_recv()
            else:
                z_arrival(k, d).wait_recv()

    def z_start(k, carry):
        for d in range(1, nz):
            when_direct(d, z_copy(k, d).start)
        return carry

    def r_copy(d):
        return remote(rbuf.at[me], rbuf.at[me], rsend.at[d], rrecv.at[me], lax.rem(me + d, n))

    def r_arrival(d):
        src = lax.rem(me + d, n)
        return remote(rbuf.at[src], rbuf.at[src], rsend.at[d], rrecv.at[src], src)

    lax.fori_loop(0, heads, z_start, 0)

    def r_start(d, carry):
        r_copy(d).start()
        return carry

    lax.fori_loop(1, n, r_start, 0)

    def c_copy(k):
        return remote(col.at[k, 0], col.at[k, 1], csend.at[k], crecv.at[k], core_peer)

    def y_copy(k):
        return remote(pbuf.at[k], ybuf.at[k], ysend.at[k], yrecv.at[k], y_peer)

    def pick(k, codes, bases):
        tiles = list(bases)
        for c in range(2):
            for z in range(nz):
                for r in range(KEEP):
                    entry = col[k, c, z, r]
                    slot = (c * nz + z) * KEEP + r
                    tiles = [
                        jnp.where(code == slot, entry, tile)
                        for code, tile in zip(codes, tiles)
                    ]
        return tiles

    def exchange_one(k):
        z_wait(k)
        c_copy(k).start()

    def exchange_two(k):
        c_copy(k).wait_recv()
        if ny > 1:
            codes = [idx[KEEP + local + j] for j in range(local)]
            tiles = pick(k, codes, [col[k, 0, 0, 0]] * local)
            for j in range(local):
                pbuf[k, j] = tiles[j]
            y_copy(k).start()

    def place(k):
        if ny > 1:
            y_copy(k).wait_recv()
        bases = [ybuf[k, j] if ny > 1 else col[k, 0, 0, 0] for j in range(local)]
        tiles = pick(k, [idx[KEEP + j] for j in range(local)], bases)
        for j in range(local):
            kbuf[k, j, new_len:] = tiles[j][0]
            vbuf[k, j, new_len:] = tiles[j][1]

    row = lax.rem(lax.broadcasted_iota(jnp.int32, (group * half, half), 0), half)
    column = lax.broadcasted_iota(jnp.int32, (group * half, half), 1)
    visible = column <= row
    scale = HEAD_SIZE ** (-0.5) * LOG2E

    def attend(k, j):
        for part in range(2):
            start = half if part == 0 else 0
            keys = kbuf[k, j, start:]
            values = vbuf[k, j, start:]
            values = jnp.concatenate([values, jnp.ones_like(values)], axis=1)
            rows = slice(part * half, (part + 1) * half)
            query = jnp.concatenate(
                [
                    qbuf[k, j, rows, g * HEAD_SIZE:(g + 1) * HEAD_SIZE]
                    for g in range(group)
                ],
                axis=0,
            )
            s = lax.dot_general(
                query, keys, (((1,), (1,)), ((), ())), preferred_element_type=jnp.float32
            )
            s = jnp.concatenate(
                [jnp.where(visible, s[:, :half], -jnp.inf), s[:, half:]], axis=1
            )
            top = jnp.max(s, axis=1, keepdims=True)
            p = jnp.exp2((s - top) * scale).astype(jnp.bfloat16)
            o = jnp.dot(p, values, preferred_element_type=jnp.float32)
            o = (o[:, :HEAD_SIZE] / o[:, HEAD_SIZE:]).astype(jnp.bfloat16)
            for g in range(group):
                obuf[k, j, rows, g * HEAD_SIZE:(g + 1) * HEAD_SIZE] = o[
                    g * half:(g + 1) * half
                ]

    def o_copy(k):
        wide = pl.ds(pl.multiple_of(k * width, width), width)
        return pltpu.make_async_copy(obuf.at[k], out_hbm.at[:, :, wide], osem.at[k])

    def attend_some(k, first, last):
        def one(j, carry):
            attend(k, j)
            return carry

        lax.fori_loop(first, last, one, 0, unroll=True)

    def ready(k):
        for copy in loads(k):
            copy.wait()
        place(k)

    def finish_head(k):
        attend_some(k, local // 2, local)
        o_copy(k).start()

    def start_head(k):
        ready(k)
        attend_some(k, 0, local // 2)

    relay(0)
    exchange_one(0)
    relay(1)
    exchange_one(1)
    exchange_two(0)
    relay(2)

    def step(k, carry):
        exchange_one(k)
        exchange_two(k - 1)
        start_head(k - 2)
        pl.when(k + 1 < heads)(functools.partial(relay, k + 1))
        finish_head(k - 2)
        return carry

    lax.fori_loop(2, heads, step, 0)
    exchange_two(heads - 1)
    for k in (heads - 2, heads - 1):
        start_head(k)
        finish_head(k)

    def finish(k, carry):
        o_copy(k).wait()
        for d in range(1, nz):
            when_direct(d, z_copy(k, d).wait_send)
        for who, source, target in ends:
            pl.when(my_z == who)(relay_copy(k, source, target).wait_send)
        c_copy(k).wait_send()
        if ny > 1:
            y_copy(k).wait_send()
        return carry

    lax.fori_loop(0, heads, finish, 0)

    def r_finish(d, carry):
        r_arrival(d).wait_recv()
        r_copy(d).wait_send()
        return carry

    lax.fori_loop(1, n, r_finish, 0)


def body(queries, new_keys, new_values, step_kv, prm_last, value_head, parents):
    n = lax.axis_size("beam")
    ny = 2 if n == 16 else 1
    nz = n // (2 * ny)
    me = lax.axis_index("beam")
    local, new_len, qwidth = queries.shape
    children = parents.shape[0]
    step_len, kv_width = step_kv.shape[2:]
    heads = kv_width // HEAD_SIZE
    width = qwidth // heads

    beams = jnp.arange(n * local, dtype=jnp.int32)
    equal = parents[None, :] == beams[:, None]
    hits = jnp.sum(equal.astype(jnp.int32), axis=1)
    kept = (hits > 0).astype(jnp.int32)
    before = jnp.sum(kept[None, :] * (beams[None, :] < beams[:, None]), axis=1)
    rank_of_beam = before % KEEP
    wanted = (
        (beams[None, :] // local == me)
        & (kept[None, :] > 0)
        & (rank_of_beam[None, :] == jnp.arange(KEEP, dtype=jnp.int32)[:, None])
    )
    keep_pos = jnp.sum(wanted * (beams % local)[None, :], axis=1).astype(jnp.int32)
    rank = jnp.sum(equal * rank_of_beam[:, None], axis=0)
    owner = parents // local
    c, y, z = owner % 2, (owner // 2) % ny, owner // (2 * ny)
    my_c, my_y = me % 2, (me // 2) % ny
    code = jnp.where(y == my_y, ((c != my_c) * nz + z) * KEEP + rank, -1).astype(jnp.int32)
    y_peer = me + 2 - 4 * my_y if ny > 1 else me
    own = lax.dynamic_slice_in_dim(code, me * local, local)
    other = lax.dynamic_slice_in_dim(code, y_peer * local, local)
    idx = jnp.concatenate([keep_pos, own, other])

    dma = pltpu.SemaphoreType.DMA
    bf16 = jnp.bfloat16
    vmem = pl.BlockSpec(memory_space=pltpu.VMEM)
    anywhere = pl.BlockSpec(memory_space=pl.ANY)
    attended, rewards = pl.pallas_call(
        functools.partial(kernel, n, ny, nz),
        out_shape=(
            jax.ShapeDtypeStruct(queries.shape, bf16),
            jax.ShapeDtypeStruct((n, local, 128), jnp.float32),
        ),
        in_specs=[pl.BlockSpec(memory_space=pltpu.SMEM), vmem, vmem, vmem]
        + [anywhere] * 3,
        out_specs=(anywhere, vmem),
        scratch_shapes=[
            pltpu.VMEM((heads, 2, nz, KEEP, 2, step_len, HEAD_SIZE), bf16),
            pltpu.VMEM((heads, local, 2, step_len, HEAD_SIZE), bf16),
            pltpu.VMEM((heads, local, 2, step_len, HEAD_SIZE), bf16),
            pltpu.VMEM((heads, local, new_len, width), bf16),
            pltpu.VMEM((heads, local, new_len + step_len, HEAD_SIZE), bf16),
            pltpu.VMEM((heads, local, new_len + step_len, HEAD_SIZE), bf16),
            pltpu.VMEM((heads, local, new_len, width), bf16),
            dma((n,)), dma((n,)),
            dma((heads, nz)), dma((heads, nz)), dma((heads,)),
            dma((heads,)), dma((heads,)),
            dma((heads,)), dma((heads,)),
            dma((heads, 5)), dma((heads,)),
        ],
        compiler_params=pltpu.CompilerParams(
            collective_id=0, has_side_effects=True, vmem_limit_bytes=56 << 20
        ),
    )(idx, prm_last, value_head.reshape(1, -1), step_kv, queries, new_keys, new_values)

    reward = rewards[:, :, 0].reshape(-1)
    total = jnp.sum(reward * hits.astype(jnp.float32))
    mine = lax.dynamic_slice_in_dim(parents, me * local, local)
    match = mine[:, None] == beams[None, :]
    child_reward = jnp.sum(jnp.where(match, reward[None, :], 0.0), axis=1)
    child_share = children * child_reward / total
    return (attended, child_share)


def solution(mesh):
    in_specs = (
        P(("prompts", "beam"), None, None),
        P(("prompts", "beam"), None, None),
        P(("prompts", "beam"), None, None),
        P(("prompts", "beam"), None, None, None),
        P(("prompts", "beam"), None),
        P(),
        P("prompts"),
    )
    out_specs = (P(("prompts", "beam"), None, None), P(("prompts", "beam")))
    return jax.shard_map(body, mesh=mesh, in_specs=in_specs, out_specs=out_specs, check_vma=False)
```

```python
import functools

import jax
import jax.numpy as jnp
from jax import lax
from jax.experimental import pallas as pl
from jax.experimental.pallas import tpu as pltpu
from jax.sharding import PartitionSpec as P

HEAD_SIZE = 128
KEEP = 2
LOG2E = 1.4426950408889634


def remote(src, dst, send, recv, device):
    return pltpu.make_async_remote_copy(
        src_ref=src, dst_ref=dst, send_sem=send, recv_sem=recv,
        device_id={"beam": device}, device_id_type=pl.DeviceIdType.MESH,
    )


def loads(k, head, hbm, buf, isem):
    q_hbm, nk_hbm, nv_hbm = hbm
    qbuf, kbuf, vbuf, _ = buf
    width = qbuf.shape[3]
    half = q_hbm.shape[1] // 2
    cols = pl.ds(pl.multiple_of(head * HEAD_SIZE, HEAD_SIZE), HEAD_SIZE)
    wide = pl.ds(pl.multiple_of(head * width, width), width)
    lo, hi = pl.ds(0, half), pl.ds(half, half)
    return [
        pltpu.make_async_copy(q_hbm.at[:, :, wide], qbuf.at[k], isem.at[k, 0]),
        pltpu.make_async_copy(nk_hbm.at[:, hi, cols], kbuf.at[k, :, lo], isem.at[k, 1]),
        pltpu.make_async_copy(nk_hbm.at[:, lo, cols], kbuf.at[k, :, hi], isem.at[k, 2]),
        pltpu.make_async_copy(nv_hbm.at[:, hi, cols], vbuf.at[k, :, lo], isem.at[k, 3]),
        pltpu.make_async_copy(nv_hbm.at[:, lo, cols], vbuf.at[k, :, hi], isem.at[k, 4]),
    ]


def store(k, head, obuf, out_hbm, osem):
    width = obuf.shape[3]
    wide = pl.ds(pl.multiple_of(head * width, width), width)
    return pltpu.make_async_copy(obuf.at[k], out_hbm.at[:, :, wide], osem.at[k])


def attend(k, j, buf):
    qbuf, kbuf, vbuf, obuf = buf
    half = qbuf.shape[2] // 2
    group = qbuf.shape[3] // HEAD_SIZE
    row = lax.rem(lax.broadcasted_iota(jnp.int32, (group * half, half), 0), half)
    column = lax.broadcasted_iota(jnp.int32, (group * half, half), 1)
    visible = column <= row
    scale = HEAD_SIZE ** (-0.5) * LOG2E
    for part in range(2):
        start = half if part == 0 else 0
        keys = kbuf[k, j, start:]
        values = vbuf[k, j, start:]
        values = jnp.concatenate([values, jnp.ones_like(values)], axis=1)
        rows = slice(part * half, (part + 1) * half)
        query = jnp.concatenate(
            [qbuf[k, j, rows, g * HEAD_SIZE:(g + 1) * HEAD_SIZE] for g in range(group)],
            axis=0,
        )
        s = lax.dot_general(
            query, keys, (((1,), (1,)), ((), ())), preferred_element_type=jnp.float32
        )
        s = jnp.concatenate(
            [jnp.where(visible, s[:, :half], -jnp.inf), s[:, half:]], axis=1
        )
        top = jnp.max(s, axis=1, keepdims=True)
        p = jnp.exp2((s - top) * scale).astype(jnp.bfloat16)
        o = jnp.dot(p, values, preferred_element_type=jnp.float32)
        o = (o[:, :HEAD_SIZE] / o[:, HEAD_SIZE:]).astype(jnp.bfloat16)
        for g in range(group):
            obuf[k, j, rows, g * HEAD_SIZE:(g + 1) * HEAD_SIZE] = o[
                g * half:(g + 1) * half
            ]


def last_kernel(
    first, tail, part, q_hbm, nk_hbm, nv_hbm, out_hbm,
    qbuf, kbuf, vbuf, obuf, held, isem, osem, hin, hout,
):
    hbm = (q_hbm, nk_hbm, nv_hbm)
    buf = (qbuf, kbuf, vbuf, obuf)
    local, new_len, done = held.shape
    count = qbuf.shape[0]

    def fetch(j):
        return pltpu.make_async_copy(part.at[j], held.at[j], hin.at[j])

    def put(j):
        return pltpu.make_async_copy(
            held.at[j], out_hbm.at[j, :, pl.ds(0, done)], hout.at[j]
        )

    for k in range(count):
        for copy in loads(k, first + k, hbm, buf, isem):
            copy.start()
        if k == 0:
            for j in range(local):
                fetch(j).start()
    for k in range(count):
        for j in range(local):
            kbuf[k, j, new_len:] = tail[k, j, 0]
            vbuf[k, j, new_len:] = tail[k, j, 1]
    for k in range(count):
        for copy in loads(k, first + k, hbm, buf, isem):
            copy.wait()
        if k > 0:
            for j in range(local):
                fetch(j).wait()
                put(j).start()

        def one(j, carry):
            attend(k, j, buf)
            return carry

        lax.fori_loop(0, local, one, 0, unroll=2)
        store(k, first + k, obuf, out_hbm, osem).start()
    for j in range(local):
        put(j).wait()
    for k in range(count):
        store(k, first + k, obuf, out_hbm, osem).wait()


def kernel(
    n, ny, nz, idx, prm, head, kv, q_hbm, nk_hbm, nv_hbm, out_hbm, rbuf, tail,
    col, pbuf, ybuf, qbuf, kbuf, vbuf, obuf,
    rsend, rrecv, zsend, zrecv, lsend, csend, crecv, ysend, yrecv, isem, osem,
):
    me = lax.axis_index("beam")
    my_c = lax.rem(me, 2)
    my_y = lax.rem(lax.div(me, 2), ny)
    my_z = lax.div(me, 2 * ny)
    local = kv.shape[0]
    step_len = kv.shape[2]
    heads = kv.shape[3] // HEAD_SIZE
    new_len = q_hbm.shape[1]
    front = qbuf.shape[0]
    hbm = (q_hbm, nk_hbm, nv_hbm)
    buf = (qbuf, kbuf, vbuf, obuf)

    def at(z, y, c):
        return (z * ny + y) * 2 + c

    core_peer = at(my_z, my_y, 1 - my_c)
    y_peer = at(my_z, lax.rem(my_y + 1, ny), my_c)

    barrier = pltpu.get_barrier_semaphore()

    def greet(d, carry):
        pl.semaphore_signal(
            barrier, inc=1, device_id={"beam": lax.rem(me + d, n)},
            device_id_type=pl.DeviceIdType.MESH,
        )
        return carry

    lax.fori_loop(1, n, greet, 0)

    def load(k, carry):
        for copy in loads(k, k, hbm, buf, isem):
            copy.start()
        return carry

    lax.fori_loop(0, front, load, 0)

    for k in range(heads):
        cols = slice(k * HEAD_SIZE, (k + 1) * HEAD_SIZE)
        for r in range(KEEP):
            tile = kv[0, :, :, cols]
            for b in range(1, local):
                tile = jnp.where(idx[r] == b, kv[b, :, :, cols], tile)
            col[k, 0, my_z, r] = tile

    hidden = prm[...].astype(jnp.float32)
    square = jnp.mean(hidden * hidden, axis=-1, keepdims=True)
    normed = hidden * lax.rsqrt(square + 1e-05)
    score = jnp.sum(normed * head[...], axis=-1, keepdims=True)
    reward = (1.0 / (1.0 + jnp.exp(-score))).astype(jnp.bfloat16).astype(jnp.float32)
    rbuf[me] = jnp.broadcast_to(reward, (local, 128))

    pl.semaphore_wait(barrier, n - 1)

    def z_copy(k, d):
        zt = lax.rem(my_z + d, nz)
        return remote(
            col.at[k, 0, my_z], col.at[k, 0, my_z],
            zsend.at[k, d], zrecv.at[k, my_z], at(zt, my_y, my_c),
        )

    def z_arrival(k, d):
        zs = lax.rem(my_z + d, nz)
        return remote(
            col.at[k, 0, zs], col.at[k, 0, zs],
            zsend.at[k, d], zrecv.at[k, zs], at(zs, my_y, my_c),
        )

    relayed = nz == 4

    def when_direct(d, run):
        if relayed and d == 1:
            pl.when(my_z != nz - 1)(run)
        elif relayed and d == nz - 1:
            pl.when(my_z != 0)(run)
        else:
            run()

    def relay_copy(k, source, target):
        return remote(
            col.at[k, 0, source], col.at[k, 0, source],
            lsend.at[k], zrecv.at[k, source], at(target, my_y, my_c),
        )

    ends = ((nz - 2, 0, nz - 1), (1, nz - 1, 0)) if relayed else ()

    def relay(k):
        for who, source, target in ends:

            @pl.when(my_z == who)
            def _():
                relay_copy(k, source, target).wait_recv()
                relay_copy(k, source, target).start()

    def z_wait(k):
        for d in range(1, nz):
            zs = lax.rem(my_z + d, nz)
            got = (my_z == 1) & (zs == nz - 1) | (my_z == nz - 2) & (zs == 0)
            if relayed:

                @pl.when(jnp.logical_not(got))
                def _():
                    z_arrival(k, d).wait_recv()
            else:
                z_arrival(k, d).wait_recv()

    def z_start(k, carry):
        for d in range(1, nz):
            when_direct(d, z_copy(k, d).start)
        return carry

    def r_copy(d):
        return remote(rbuf.at[me], rbuf.at[me], rsend.at[d], rrecv.at[me], lax.rem(me + d, n))

    def r_arrival(d):
        src = lax.rem(me + d, n)
        return remote(rbuf.at[src], rbuf.at[src], rsend.at[d], rrecv.at[src], src)

    lax.fori_loop(0, heads, z_start, 0)

    def r_start(d, carry):
        r_copy(d).start()
        return carry

    lax.fori_loop(1, n, r_start, 0)

    def c_copy(k):
        return remote(col.at[k, 0], col.at[k, 1], csend.at[k], crecv.at[k], core_peer)

    def y_copy(k):
        return remote(pbuf.at[k], ybuf.at[k], ysend.at[k], yrecv.at[k], y_peer)

    def pick(k, codes, bases):
        tiles = list(bases)
        for c in range(2):
            for z in range(nz):
                for r in range(KEEP):
                    entry = col[k, c, z, r]
                    slot = (c * nz + z) * KEEP + r
                    tiles = [
                        jnp.where(code == slot, entry, tile)
                        for code, tile in zip(codes, tiles)
                    ]
        return tiles

    def exchange_one(k):
        z_wait(k)
        c_copy(k).start()

    def exchange_two(k):
        c_copy(k).wait_recv()
        if ny > 1:
            codes = [idx[KEEP + local + j] for j in range(local)]
            tiles = pick(k, codes, [col[k, 0, 0, 0]] * local)
            for j in range(local):
                pbuf[k, j] = tiles[j]
            y_copy(k).start()

    def parents_of(k):
        if ny > 1:
            y_copy(k).wait_recv()
        bases = [ybuf[k, j] if ny > 1 else col[k, 0, 0, 0] for j in range(local)]
        return pick(k, [idx[KEEP + j] for j in range(local)], bases)

    def place(k):
        tiles = parents_of(k)
        for j in range(local):
            kbuf[k, j, new_len:] = tiles[j][0]
            vbuf[k, j, new_len:] = tiles[j][1]

    def attend_some(k, first, last):
        def one(j, carry):
            attend(k, j, buf)
            return carry

        lax.fori_loop(first, last, one, 0, unroll=True)

    def ready(k):
        for copy in loads(k, k, hbm, buf, isem):
            copy.wait()
        place(k)

    def finish_head(k):
        attend_some(k, local // 2, local)
        store(k, k, obuf, out_hbm, osem).start()

    def start_head(k):
        ready(k)
        attend_some(k, 0, local // 2)

    relay(0)
    exchange_one(0)
    relay(1)
    exchange_one(1)
    exchange_two(0)
    relay(2)

    def step(k, carry):
        exchange_one(k)
        exchange_two(k - 1)
        start_head(k - 2)
        pl.when(k + 1 < heads)(functools.partial(relay, k + 1))
        finish_head(k - 2)
        return carry

    lax.fori_loop(2, heads, step, 0)
    exchange_two(heads - 1)
    for k in range(front, heads):
        tiles = parents_of(k)
        for j in range(local):
            tail[k - front, j] = tiles[j]

    def finish(k, carry):
        for d in range(1, nz):
            when_direct(d, z_copy(k, d).wait_send)
        for who, source, target in ends:
            pl.when(my_z == who)(relay_copy(k, source, target).wait_send)
        c_copy(k).wait_send()
        if ny > 1:
            y_copy(k).wait_send()
        return carry

    lax.fori_loop(0, heads, finish, 0)

    def stored(k, carry):
        store(k, k, obuf, out_hbm, osem).wait()
        return carry

    lax.fori_loop(0, front, stored, 0)

    def r_finish(d, carry):
        r_arrival(d).wait_recv()
        r_copy(d).wait_send()
        return carry

    lax.fori_loop(1, n, r_finish, 0)


def body(queries, new_keys, new_values, step_kv, prm_last, value_head, parents):
    n = lax.axis_size("beam")
    ny = 2 if n == 16 else 1
    nz = n // (2 * ny)
    me = lax.axis_index("beam")
    local, new_len, qwidth = queries.shape
    children = parents.shape[0]
    step_len, kv_width = step_kv.shape[2:]
    heads = kv_width // HEAD_SIZE
    width = qwidth // heads

    beams = jnp.arange(n * local, dtype=jnp.int32)
    equal = parents[None, :] == beams[:, None]
    hits = jnp.sum(equal.astype(jnp.int32), axis=1)
    kept = (hits > 0).astype(jnp.int32)
    before = jnp.sum(kept[None, :] * (beams[None, :] < beams[:, None]), axis=1)
    rank_of_beam = before % KEEP
    wanted = (
        (beams[None, :] // local == me)
        & (kept[None, :] > 0)
        & (rank_of_beam[None, :] == jnp.arange(KEEP, dtype=jnp.int32)[:, None])
    )
    keep_pos = jnp.sum(wanted * (beams % local)[None, :], axis=1).astype(jnp.int32)
    rank = jnp.sum(equal * rank_of_beam[:, None], axis=0)
    owner = parents // local
    c, y, z = owner % 2, (owner // 2) % ny, owner // (2 * ny)
    my_c, my_y = me % 2, (me // 2) % ny
    code = jnp.where(y == my_y, ((c != my_c) * nz + z) * KEEP + rank, -1).astype(jnp.int32)
    y_peer = me + 2 - 4 * my_y if ny > 1 else me
    own = lax.dynamic_slice_in_dim(code, me * local, local)
    other = lax.dynamic_slice_in_dim(code, y_peer * local, local)
    idx = jnp.concatenate([keep_pos, own, other])

    dma = pltpu.SemaphoreType.DMA
    bf16 = jnp.bfloat16
    vmem = pl.BlockSpec(memory_space=pltpu.VMEM)
    anywhere = pl.BlockSpec(memory_space=pl.ANY)
    last = 2
    front = heads - last
    part, rewards, tail = pl.pallas_call(
        functools.partial(kernel, n, ny, nz),
        out_shape=(
            jax.ShapeDtypeStruct((local, new_len, front * width), bf16),
            jax.ShapeDtypeStruct((n, local, 128), jnp.float32),
            jax.ShapeDtypeStruct((last, local, 2, step_len, HEAD_SIZE), bf16),
        ),
        in_specs=[pl.BlockSpec(memory_space=pltpu.SMEM), vmem, vmem, vmem]
        + [anywhere] * 3,
        out_specs=(anywhere, vmem, vmem),
        scratch_shapes=[
            pltpu.VMEM((heads, 2, nz, KEEP, 2, step_len, HEAD_SIZE), bf16),
            pltpu.VMEM((heads, local, 2, step_len, HEAD_SIZE), bf16),
            pltpu.VMEM((heads, local, 2, step_len, HEAD_SIZE), bf16),
            pltpu.VMEM((front, local, new_len, width), bf16),
            pltpu.VMEM((front, local, new_len + step_len, HEAD_SIZE), bf16),
            pltpu.VMEM((front, local, new_len + step_len, HEAD_SIZE), bf16),
            pltpu.VMEM((front, local, new_len, width), bf16),
            dma((n,)), dma((n,)),
            dma((heads, nz)), dma((heads, nz)), dma((heads,)),
            dma((heads,)), dma((heads,)),
            dma((heads,)), dma((heads,)),
            dma((front, 5)), dma((front,)),
        ],
        compiler_params=pltpu.CompilerParams(
            collective_id=0, has_side_effects=True, vmem_limit_bytes=56 << 20
        ),
    )(idx, prm_last, value_head.reshape(1, -1), step_kv, queries, new_keys, new_values)

    attended = pl.pallas_call(
        functools.partial(last_kernel, front),
        out_shape=jax.ShapeDtypeStruct(queries.shape, bf16),
        in_specs=[vmem] + [anywhere] * 4,
        out_specs=anywhere,
        scratch_shapes=[
            pltpu.VMEM((last, local, new_len, width), bf16),
            pltpu.VMEM((last, local, new_len + step_len, HEAD_SIZE), bf16),
            pltpu.VMEM((last, local, new_len + step_len, HEAD_SIZE), bf16),
            pltpu.VMEM((last, local, new_len, width), bf16),
            pltpu.VMEM((local, new_len, front * width), bf16),
            dma((last, 5)), dma((last,)), dma((local,)), dma((local,)),
        ],
        compiler_params=pltpu.CompilerParams(vmem_limit_bytes=56 << 20),
    )(tail, part, queries, new_keys, new_values)

    reward = rewards[:, :, 0].reshape(-1)
    total = jnp.sum(reward * hits.astype(jnp.float32))
    mine = lax.dynamic_slice_in_dim(parents, me * local, local)
    match = mine[:, None] == beams[None, :]
    child_reward = jnp.sum(jnp.where(match, reward[None, :], 0.0), axis=1)
    child_share = children * child_reward / total
    return (attended, child_share)


def solution(mesh):
    in_specs = (
        P(("prompts", "beam"), None, None),
        P(("prompts", "beam"), None, None),
        P(("prompts", "beam"), None, None),
        P(("prompts", "beam"), None, None, None),
        P(("prompts", "beam"), None),
        P(),
        P("prompts"),
    )
    out_specs = (P(("prompts", "beam"), None, None), P(("prompts", "beam")))
    return jax.shard_map(body, mesh=mesh, in_specs=in_specs, out_specs=out_specs, check_vma=False)
```

```python
import functools

import jax
import jax.numpy as jnp
from jax import lax
from jax.experimental import pallas as pl
from jax.experimental.pallas import tpu as pltpu
from jax.sharding import PartitionSpec as P

HEAD_SIZE = 128
KEEP = 2
LOG2E = 1.4426950408889634


def remote(src, dst, send, recv, device):
    return pltpu.make_async_remote_copy(
        src_ref=src, dst_ref=dst, send_sem=send, recv_sem=recv,
        device_id={"beam": device}, device_id_type=pl.DeviceIdType.MESH,
    )


def loads(k, head, hbm, buf, isem):
    q_hbm, nk_hbm, nv_hbm = hbm
    qbuf, kbuf, vbuf, _ = buf
    width = qbuf.shape[3]
    half = q_hbm.shape[1] // 2
    cols = pl.ds(pl.multiple_of(head * HEAD_SIZE, HEAD_SIZE), HEAD_SIZE)
    wide = pl.ds(pl.multiple_of(head * width, width), width)
    lo, hi = pl.ds(0, half), pl.ds(half, half)
    return [
        pltpu.make_async_copy(q_hbm.at[:, :, wide], qbuf.at[k], isem.at[k, 0]),
        pltpu.make_async_copy(nk_hbm.at[:, hi, cols], kbuf.at[k, :, lo], isem.at[k, 1]),
        pltpu.make_async_copy(nk_hbm.at[:, lo, cols], kbuf.at[k, :, hi], isem.at[k, 2]),
        pltpu.make_async_copy(nv_hbm.at[:, hi, cols], vbuf.at[k, :, lo], isem.at[k, 3]),
        pltpu.make_async_copy(nv_hbm.at[:, lo, cols], vbuf.at[k, :, hi], isem.at[k, 4]),
    ]


def store(k, head, obuf, out_hbm, osem):
    width = obuf.shape[3]
    wide = pl.ds(pl.multiple_of(head * width, width), width)
    return pltpu.make_async_copy(obuf.at[k], out_hbm.at[:, :, wide], osem.at[k])


def attend(k, j, buf):
    qbuf, kbuf, vbuf, obuf = buf
    half = qbuf.shape[2] // 2
    group = qbuf.shape[3] // HEAD_SIZE
    row = lax.rem(lax.broadcasted_iota(jnp.int32, (group * half, half), 0), half)
    column = lax.broadcasted_iota(jnp.int32, (group * half, half), 1)
    visible = column <= row
    scale = HEAD_SIZE ** (-0.5) * LOG2E
    for part in range(2):
        start = half if part == 0 else 0
        keys = kbuf[k, j, start:]
        values = vbuf[k, j, start:]
        values = jnp.concatenate([values, jnp.ones_like(values)], axis=1)
        rows = slice(part * half, (part + 1) * half)
        query = jnp.concatenate(
            [qbuf[k, j, rows, g * HEAD_SIZE:(g + 1) * HEAD_SIZE] for g in range(group)],
            axis=0,
        )
        s = lax.dot_general(
            query, keys, (((1,), (1,)), ((), ())), preferred_element_type=jnp.float32
        )
        s = jnp.concatenate(
            [jnp.where(visible, s[:, :half], -jnp.inf), s[:, half:]], axis=1
        )
        top = jnp.max(s, axis=1, keepdims=True)
        p = jnp.exp2((s - top) * scale).astype(jnp.bfloat16)
        o = jnp.dot(p, values, preferred_element_type=jnp.float32)
        o = (o[:, :HEAD_SIZE] / o[:, HEAD_SIZE:]).astype(jnp.bfloat16)
        for g in range(group):
            obuf[k, j, rows, g * HEAD_SIZE:(g + 1) * HEAD_SIZE] = o[
                g * half:(g + 1) * half
            ]


def last_kernel(
    first, tail, part, q_hbm, nk_hbm, nv_hbm, out_hbm,
    qbuf, kbuf, vbuf, obuf, held, isem, osem, hin, hout,
):
    hbm = (q_hbm, nk_hbm, nv_hbm)
    buf = (qbuf, kbuf, vbuf, obuf)
    local, new_len, done = held.shape
    count = qbuf.shape[0]

    def fetch(j):
        return pltpu.make_async_copy(part.at[j], held.at[j], hin.at[j])

    def put(j):
        return pltpu.make_async_copy(
            held.at[j], out_hbm.at[j, :, pl.ds(0, done)], hout.at[j]
        )

    for k in range(count):
        for copy in loads(k, first + k, hbm, buf, isem):
            copy.start()
        if k == 0:
            for j in range(local):
                fetch(j).start()
    for k in range(count):
        for j in range(local):
            kbuf[k, j, new_len:] = tail[k, j, 0]
            vbuf[k, j, new_len:] = tail[k, j, 1]
    for k in range(count):
        for copy in loads(k, first + k, hbm, buf, isem):
            copy.wait()
        if k > 0:
            for j in range(local):
                fetch(j).wait()
                put(j).start()

        def one(j, carry):
            attend(k, j, buf)
            return carry

        lax.fori_loop(0, local, one, 0, unroll=2)
        store(k, first + k, obuf, out_hbm, osem).start()
    for j in range(local):
        put(j).wait()
    for k in range(count):
        store(k, first + k, obuf, out_hbm, osem).wait()


def kernel(
    n, ny, nz, idx, prm, head, kv, q_hbm, nk_hbm, nv_hbm, out_hbm, rbuf, tail,
    col, pbuf, ybuf, qbuf, kbuf, vbuf, obuf,
    rsend, rrecv, zsend, zrecv, lsend, csend, crecv, ysend, yrecv, isem, osem,
):
    me = lax.axis_index("beam")
    my_c = lax.rem(me, 2)
    my_y = lax.rem(lax.div(me, 2), ny)
    my_z = lax.div(me, 2 * ny)
    local = kv.shape[0]
    step_len = kv.shape[2]
    heads = kv.shape[3] // HEAD_SIZE
    new_len = q_hbm.shape[1]
    front = qbuf.shape[0]
    hbm = (q_hbm, nk_hbm, nv_hbm)
    buf = (qbuf, kbuf, vbuf, obuf)

    def at(z, y, c):
        return (z * ny + y) * 2 + c

    core_peer = at(my_z, my_y, 1 - my_c)
    y_peer = at(my_z, lax.rem(my_y + 1, ny), my_c)

    barrier = pltpu.get_barrier_semaphore()

    def greet(d, carry):
        pl.semaphore_signal(
            barrier, inc=1, device_id={"beam": lax.rem(me + d, n)},
            device_id_type=pl.DeviceIdType.MESH,
        )
        return carry

    lax.fori_loop(1, n, greet, 0)

    def load(k, carry):
        for copy in loads(k, k, hbm, buf, isem):
            copy.start()
        return carry

    lax.fori_loop(0, front, load, 0)

    for k in range(heads):
        cols = slice(k * HEAD_SIZE, (k + 1) * HEAD_SIZE)
        for r in range(KEEP):
            tile = kv[0, :, :, cols]
            for b in range(1, local):
                tile = jnp.where(idx[r] == b, kv[b, :, :, cols], tile)
            col[k, 0, my_z, r] = tile

    hidden = prm[...].astype(jnp.float32)
    square = jnp.mean(hidden * hidden, axis=-1, keepdims=True)
    normed = hidden * lax.rsqrt(square + 1e-05)
    score = jnp.sum(normed * head[...], axis=-1, keepdims=True)
    reward = (1.0 / (1.0 + jnp.exp(-score))).astype(jnp.bfloat16).astype(jnp.float32)
    rbuf[me] = jnp.broadcast_to(reward, (local, 128))

    pl.semaphore_wait(barrier, n - 1)

    def z_copy(k, d):
        zt = lax.rem(my_z + d, nz)
        return remote(
            col.at[k, 0, my_z], col.at[k, 0, my_z],
            zsend.at[k, d], zrecv.at[k, my_z], at(zt, my_y, my_c),
        )

    def z_arrival(k, d):
        zs = lax.rem(my_z + d, nz)
        return remote(
            col.at[k, 0, zs], col.at[k, 0, zs],
            zsend.at[k, d], zrecv.at[k, zs], at(zs, my_y, my_c),
        )

    relayed = nz == 4

    def when_direct(d, run):
        if relayed and d == 1:
            pl.when(my_z != nz - 1)(run)
        elif relayed and d == nz - 1:
            pl.when(my_z != 0)(run)
        else:
            run()

    def relay_copy(k, source, target):
        return remote(
            col.at[k, 0, source], col.at[k, 0, source],
            lsend.at[k], zrecv.at[k, source], at(target, my_y, my_c),
        )

    ends = ((nz - 2, 0, nz - 1), (1, nz - 1, 0)) if relayed else ()

    def relay(k):
        for who, source, target in ends:

            @pl.when(my_z == who)
            def _():
                relay_copy(k, source, target).wait_recv()
                relay_copy(k, source, target).start()

    def z_wait(k):
        for d in range(1, nz):
            zs = lax.rem(my_z + d, nz)
            got = (my_z == 1) & (zs == nz - 1) | (my_z == nz - 2) & (zs == 0)
            if relayed:

                @pl.when(jnp.logical_not(got))
                def _():
                    z_arrival(k, d).wait_recv()
            else:
                z_arrival(k, d).wait_recv()

    def z_start(k, carry):
        for d in range(1, nz):
            when_direct(d, z_copy(k, d).start)
        return carry

    def r_copy(d):
        return remote(rbuf.at[me], rbuf.at[me], rsend.at[d], rrecv.at[me], lax.rem(me + d, n))

    def r_arrival(d):
        src = lax.rem(me + d, n)
        return remote(rbuf.at[src], rbuf.at[src], rsend.at[d], rrecv.at[src], src)

    lax.fori_loop(0, heads, z_start, 0)

    def r_start(d, carry):
        r_copy(d).start()
        return carry

    lax.fori_loop(1, n, r_start, 0)

    def c_copy(k):
        return remote(col.at[k, 0], col.at[k, 1], csend.at[k], crecv.at[k], core_peer)

    def y_copy(k):
        return remote(pbuf.at[k], ybuf.at[k], ysend.at[k], yrecv.at[k], y_peer)

    def pick(k, codes, bases):
        tiles = list(bases)
        for c in range(2):
            for z in range(nz):
                for r in range(KEEP):
                    entry = col[k, c, z, r]
                    slot = (c * nz + z) * KEEP + r
                    tiles = [
                        jnp.where(code == slot, entry, tile)
                        for code, tile in zip(codes, tiles)
                    ]
        return tiles

    def exchange_one(k):
        z_wait(k)
        c_copy(k).start()

    def exchange_two(k):
        c_copy(k).wait_recv()
        if ny > 1:
            codes = [idx[KEEP + local + j] for j in range(local)]
            tiles = pick(k, codes, [col[k, 0, 0, 0]] * local)
            for j in range(local):
                pbuf[k, j] = tiles[j]
            y_copy(k).start()

    def parents_of(k):
        if ny > 1:
            y_copy(k).wait_recv()
        bases = [ybuf[k, j] if ny > 1 else col[k, 0, 0, 0] for j in range(local)]
        return pick(k, [idx[KEEP + j] for j in range(local)], bases)

    def place(k):
        tiles = parents_of(k)
        for j in range(local):
            kbuf[k, j, new_len:] = tiles[j][0]
            vbuf[k, j, new_len:] = tiles[j][1]

    def attend_some(k, first, last):
        def one(j, carry):
            attend(k, j, buf)
            return carry

        lax.fori_loop(first, last, one, 0, unroll=True)

    def ready(k):
        for copy in loads(k, k, hbm, buf, isem):
            copy.wait()
        place(k)

    def finish_head(k):
        attend_some(k, local // 2, local)
        store(k, k, obuf, out_hbm, osem).start()

    def start_head(k):
        ready(k)
        attend_some(k, 0, local // 2)

    relay(0)
    exchange_one(0)
    relay(1)
    exchange_one(1)
    exchange_two(0)
    relay(2)

    def step(k, carry):
        exchange_one(k)
        exchange_two(k - 1)
        pl.when(k + 1 < heads)(functools.partial(relay, k + 1))
        start_head(k - 2)
        finish_head(k - 2)
        return carry

    lax.fori_loop(2, heads, step, 0)
    exchange_two(heads - 1)
    for k in range(front, heads):
        tiles = parents_of(k)
        for j in range(local):
            tail[k - front, j] = tiles[j]

    def finish(k, carry):
        for d in range(1, nz):
            when_direct(d, z_copy(k, d).wait_send)
        for who, source, target in ends:
            pl.when(my_z == who)(relay_copy(k, source, target).wait_send)
        c_copy(k).wait_send()
        if ny > 1:
            y_copy(k).wait_send()
        return carry

    lax.fori_loop(0, heads, finish, 0)

    def stored(k, carry):
        store(k, k, obuf, out_hbm, osem).wait()
        return carry

    lax.fori_loop(0, front, stored, 0)

    def r_finish(d, carry):
        r_arrival(d).wait_recv()
        r_copy(d).wait_send()
        return carry

    lax.fori_loop(1, n, r_finish, 0)


def body(queries, new_keys, new_values, step_kv, prm_last, value_head, parents):
    n = lax.axis_size("beam")
    ny = 2 if n == 16 else 1
    nz = n // (2 * ny)
    me = lax.axis_index("beam")
    local, new_len, qwidth = queries.shape
    children = parents.shape[0]
    step_len, kv_width = step_kv.shape[2:]
    heads = kv_width // HEAD_SIZE
    width = qwidth // heads

    beams = jnp.arange(n * local, dtype=jnp.int32)
    equal = parents[None, :] == beams[:, None]
    hits = jnp.sum(equal.astype(jnp.int32), axis=1)
    kept = (hits > 0).astype(jnp.int32)
    before = jnp.sum(kept[None, :] * (beams[None, :] < beams[:, None]), axis=1)
    rank_of_beam = before % KEEP
    wanted = (
        (beams[None, :] // local == me)
        & (kept[None, :] > 0)
        & (rank_of_beam[None, :] == jnp.arange(KEEP, dtype=jnp.int32)[:, None])
    )
    keep_pos = jnp.sum(wanted * (beams % local)[None, :], axis=1).astype(jnp.int32)
    rank = jnp.sum(equal * rank_of_beam[:, None], axis=0)
    owner = parents // local
    c, y, z = owner % 2, (owner // 2) % ny, owner // (2 * ny)
    my_c, my_y = me % 2, (me // 2) % ny
    code = jnp.where(y == my_y, ((c != my_c) * nz + z) * KEEP + rank, -1).astype(jnp.int32)
    y_peer = me + 2 - 4 * my_y if ny > 1 else me
    own = lax.dynamic_slice_in_dim(code, me * local, local)
    other = lax.dynamic_slice_in_dim(code, y_peer * local, local)
    idx = jnp.concatenate([keep_pos, own, other])

    dma = pltpu.SemaphoreType.DMA
    bf16 = jnp.bfloat16
    vmem = pl.BlockSpec(memory_space=pltpu.VMEM)
    anywhere = pl.BlockSpec(memory_space=pl.ANY)
    last = 2
    front = heads - last
    part, rewards, tail = pl.pallas_call(
        functools.partial(kernel, n, ny, nz),
        out_shape=(
            jax.ShapeDtypeStruct((local, new_len, front * width), bf16),
            jax.ShapeDtypeStruct((n, local, 128), jnp.float32),
            jax.ShapeDtypeStruct((last, local, 2, step_len, HEAD_SIZE), bf16),
        ),
        in_specs=[pl.BlockSpec(memory_space=pltpu.SMEM), vmem, vmem, vmem]
        + [anywhere] * 3,
        out_specs=(anywhere, vmem, vmem),
        scratch_shapes=[
            pltpu.VMEM((heads, 2, nz, KEEP, 2, step_len, HEAD_SIZE), bf16),
            pltpu.VMEM((heads, local, 2, step_len, HEAD_SIZE), bf16),
            pltpu.VMEM((heads, local, 2, step_len, HEAD_SIZE), bf16),
            pltpu.VMEM((front, local, new_len, width), bf16),
            pltpu.VMEM((front, local, new_len + step_len, HEAD_SIZE), bf16),
            pltpu.VMEM((front, local, new_len + step_len, HEAD_SIZE), bf16),
            pltpu.VMEM((front, local, new_len, width), bf16),
            dma((n,)), dma((n,)),
            dma((heads, nz)), dma((heads, nz)), dma((heads,)),
            dma((heads,)), dma((heads,)),
            dma((heads,)), dma((heads,)),
            dma((front, 5)), dma((front,)),
        ],
        compiler_params=pltpu.CompilerParams(
            collective_id=0, has_side_effects=True, vmem_limit_bytes=56 << 20
        ),
    )(idx, prm_last, value_head.reshape(1, -1), step_kv, queries, new_keys, new_values)

    attended = pl.pallas_call(
        functools.partial(last_kernel, front),
        out_shape=jax.ShapeDtypeStruct(queries.shape, bf16),
        in_specs=[vmem] + [anywhere] * 4,
        out_specs=anywhere,
        scratch_shapes=[
            pltpu.VMEM((last, local, new_len, width), bf16),
            pltpu.VMEM((last, local, new_len + step_len, HEAD_SIZE), bf16),
            pltpu.VMEM((last, local, new_len + step_len, HEAD_SIZE), bf16),
            pltpu.VMEM((last, local, new_len, width), bf16),
            pltpu.VMEM((local, new_len, front * width), bf16),
            dma((last, 5)), dma((last,)), dma((local,)), dma((local,)),
        ],
        compiler_params=pltpu.CompilerParams(vmem_limit_bytes=56 << 20),
    )(tail, part, queries, new_keys, new_values)

    reward = rewards[:, :, 0].reshape(-1)
    total = jnp.sum(reward * hits.astype(jnp.float32))
    mine = lax.dynamic_slice_in_dim(parents, me * local, local)
    match = mine[:, None] == beams[None, :]
    child_reward = jnp.sum(jnp.where(match, reward[None, :], 0.0), axis=1)
    child_share = children * child_reward / total
    return (attended, child_share)


def solution(mesh):
    in_specs = (
        P(("prompts", "beam"), None, None),
        P(("prompts", "beam"), None, None),
        P(("prompts", "beam"), None, None),
        P(("prompts", "beam"), None, None, None),
        P(("prompts", "beam"), None),
        P(),
        P("prompts"),
    )
    out_specs = (P(("prompts", "beam"), None, None), P(("prompts", "beam")))
    return jax.shard_map(body, mesh=mesh, in_specs=in_specs, out_specs=out_specs, check_vma=False)
```
